768 devices in a mesh: space: 64 (over z_lo, y, core), filt: 12 (over z_hi, x).
Axes of the slice: x: 4, y: 8, z: 12 (z_hi: 3, z_lo: 4; z = z_hi * 4 + z_lo), core: 2. Of those that a mesh axis runs over, the one named last changes fastest.
Arguments:
- volumes: bfloat16 [2, 48, 256, 16, 4, 128], P(None, 'filt', 'space'), may hold values from -6 to 6
- first_kernel: bfloat16 [3, 3, 3, 32, 16], replicated, may hold values from -0.3125 to 0.3125
- deep_kernel: bfloat16 [3, 3, 3, 64, 32], replicated, may hold values from -0.21875 to 0.21875
Outputs:
- deep_out: bfloat16 [64, 2, 12, 64, 128], P('space', None, 'filt')
The draws below stay inside these ranges and needn't reach their ends.
All inputs are finite; a program needn't handle non-finite values.
Results may differ from the reference program's by a relative error of at most 0.0048.
Values may be sent and summed in bfloat16 or wider, within the bound.
A program may use at most 32 MiB of HBM per device.

```python
import jax
import jax.numpy as jnp
from jax import lax

CIN = 16
C1 = 32
C2 = 64
VOL = 2
Z = 512
X = 48
Y = 256


def shard_levels(key, extent, pieces, smallest, high):
    gain, own = 1.0, jax.random.fold_in(key, 6)
    for axis_at, shards_of in pieces:
        steps = jnp.exp(jax.random.uniform(jax.random.fold_in(own, axis_at), (shards_of,), jnp.float32, smallest / len(pieces), high / len(pieces)))
        gain = gain * jnp.repeat(steps, extent[axis_at] // shards_of).reshape([-1 if axis == axis_at else 1 for axis in range(len(extent))])
    return gain


def noise(key, extent, width, bound, shards=(), dtype=jnp.bfloat16):
    result = width * jax.random.normal(key, extent, jnp.float32)
    if shards:
        result = result * shard_levels(key, extent, shards, -0.22, 0.18)
    return jnp.clip(result, -bound, bound).astype(dtype)


def setup_inputs(seed: int = 0) -> dict:
    key_of = jax.random.split(jax.random.key(seed), 4)
    volumes = noise(key_of[0], (VOL, X, Y, CIN, 4, Z // 4), 1.0, 6.0, ((1, 12), (2, 64)))
    first_kernel = noise(key_of[1], (3, 3, 3, C1, CIN), (27 * CIN) ** -0.5, 0.3125)
    deep_kernel = noise(key_of[2], (3, 3, 3, C2, C1), (27 * C1) ** -0.5, 0.21875)
    return {"volumes": volumes, "first_kernel": first_kernel, "deep_kernel": deep_kernel}


def leaky(value):
    return jnp.where(value >= 0, value, 0.3 * value)


def strided_conv(padded, kernel, count_x, count_y, count_z, form):
    total = None
    shape = padded.shape
    for tap_a in range(3):
        for tap_b in range(3):
            for tap_c in range(3):
                slab = lax.slice(padded, (0, tap_a, tap_b, 0, tap_c),
                                 (shape[0], tap_a + 2 * count_x - 1, tap_b + 2 * count_y - 1, shape[3], tap_c + 2 * count_z - 1),
                                 (1, 2, 2, 1, 2))
                term = jnp.einsum(form, kernel[tap_a, tap_b, tap_c].astype(jnp.float32), slab.astype(jnp.float32))
                total = term if total is None else total + term
    return total


def reference(volumes, first_kernel, deep_kernel):
    natural = jnp.transpose(volumes, (0, 1, 2, 3, 5, 4)).reshape(VOL, X, Y, CIN, Z)
    results = []
    for index in range(VOL):
        single = natural[index:index + 1]
        padded = jnp.pad(single, ((0, 0), (1, 0), (1, 0), (0, 0), (1, 0)))
        hidden = leaky(strided_conv(padded, first_kernel, X // 2, Y // 2, Z // 2, "oc,vxycz->vxyoz")).astype(jnp.bfloat16)
        padded_hidden = jnp.pad(hidden, ((0, 0), (1, 0), (1, 0), (0, 0), (1, 0)))
        deep = strided_conv(padded_hidden, deep_kernel, X // 4, Y // 4, Z // 4, "oc,vxycz->ovxyz")
        results.append(leaky(deep).astype(jnp.bfloat16))
    return jnp.concatenate(results, axis=1)
```

```python
import functools

import jax
import jax.numpy as jnp
from jax import lax
from jax.experimental import pallas as pl
from jax.experimental.pallas import tpu as pltpu
from jax.sharding import PartitionSpec as P

MESH = pl.DeviceIdType.MESH


def leaky(value):
    return jnp.where(value >= 0, value, 0.3 * value)


def first_weights(kernel):
    taps_x, taps_y, _, filters, channels = kernel.shape
    tap = [kernel[:, :, t] for t in range(3)]
    none = jnp.zeros_like(tap[0])
    rows = [
        jnp.stack([tap[1], tap[2], none, none], axis=-1),
        jnp.stack([none, tap[0], tap[1], tap[2]], axis=-1),
        jnp.stack([none, none, none, tap[0]], axis=-1),
    ]
    table = jnp.concatenate(rows, axis=2)
    table = table.reshape(taps_x, taps_y, 3 * filters, 4 * channels)
    return jnp.swapaxes(table, 1, 2).reshape(taps_x, 3 * filters, taps_y * 4 * channels)


def deep_weights(kernel):
    taps_x, taps_y, _, filters, channels = kernel.shape
    tap = [kernel[:, :, t] for t in range(3)]
    none = jnp.zeros_like(tap[0])
    table = jnp.concatenate(
        [jnp.concatenate([tap[1], tap[2]], axis=-1), jnp.concatenate([none, tap[0]], axis=-1)],
        axis=2,
    )
    return jnp.swapaxes(table, 1, 2).reshape(taps_x, 2 * filters, taps_y * 2 * channels)


def shift_lane(value, lanes):
    parts = []
    for start in range(0, value.shape[1], lanes):
        part = pltpu.roll(value[:, start : start + lanes], 1, 1)
        lane = lax.broadcasted_iota(jnp.int32, part.shape, 1)
        parts.append(jnp.where(lane == 0, 0.0, part))
    return jnp.concatenate(parts, axis=1)


def dot(left, right):
    return jnp.dot(left, right, preferred_element_type=jnp.float32)


def brick_kernel(
    count_space,
    count_filt,
    vol,
    first,
    deep,
    out,
    row,
    upper,
    lower,
    part_out,
    part_in,
    sum_out,
    sum_in,
    blocks_out,
    blocks_in,
    send_sem,
    recv_sem,
    block_send,
    block_recv,
):
    volumes, _, _, cells, lanes = vol.shape
    me = lax.axis_index("space")
    column = lax.axis_index("filt")
    has_left, has_right = column > 0, column < count_filt - 1
    has_down, has_up = me > 0, me < count_space - 1
    barrier = pltpu.get_barrier_semaphore()

    def greet(step, carry):
        peer = lax.rem(me + step, count_space)
        pl.semaphore_signal(barrier, inc=1, device_id={"space": peer}, device_id_type=MESH)
        return carry

    @pl.when(has_left)
    def _():
        pl.semaphore_signal(barrier, inc=1, device_id={"filt": column - 1}, device_id_type=MESH)

    @pl.when(has_right)
    def _():
        pl.semaphore_signal(barrier, inc=1, device_id={"filt": column + 1}, device_id_type=MESH)

    lax.fori_loop(1, count_space, greet, 0)

    def to_up(which, source, target):
        return pltpu.make_async_remote_copy(
            src_ref=source,
            dst_ref=target,
            send_sem=send_sem.at[which],
            recv_sem=recv_sem.at[which],
            device_id={"space": me + 1},
            device_id_type=MESH,
        )

    def to_right(which, source, target):
        return pltpu.make_async_remote_copy(
            src_ref=source,
            dst_ref=target,
            send_sem=send_sem.at[which],
            recv_sem=recv_sem.at[which],
            device_id={"filt": column + 1},
            device_id_type=MESH,
        )

    last = vol.shape[2] - 1
    row_copy = to_up(0, vol.at[:, :, last], row)
    upper_copy = to_up(1, upper.at[2], upper.at[0])
    lower_copy = to_up(2, lower.at[2], lower.at[0])
    part_copies = [to_right(3 + j, part_out.at[j], part_in.at[j]) for j in range(2)]
    sum_copy = to_right(5, sum_out, sum_in)

    @pl.when(jnp.logical_not(has_down))
    def _():
        row[...] = jnp.zeros_like(row)
        upper[0] = jnp.zeros(upper.shape[1:], upper.dtype)
        lower[0] = jnp.zeros(lower.shape[1:], lower.dtype)

    @pl.when(jnp.logical_not(has_left))
    def _():
        part_in[...] = jnp.zeros_like(part_in)
        sum_in[...] = jnp.zeros_like(sum_in)

    def slab(plane, j):
        sides = []
        for v in range(volumes):
            if j == 0:
                own = vol[v, plane, 0:2].reshape(2 * cells, lanes)
                sides.append(jnp.concatenate([row[v, plane], own], axis=0))
            else:
                sides.append(vol[v, plane, 1:4].reshape(3 * cells, lanes))
        return jnp.concatenate(sides, axis=1)

    def first_sum(value):
        third = value.shape[0] // 3
        even = value[:third] + shift_lane(value[2 * third :], lanes)
        return jnp.concatenate([even, value[third : 2 * third]], axis=0)

    def deep_sum(value):
        half = value.shape[0] // 2
        return value[:half] + shift_lane(value[half:], lanes)

    def first_layer(j):
        three = slab(3, j)
        part_out[j] = first_sum(dot(first[0], three)).astype(jnp.bfloat16)
        one = slab(1, j)
        whole = dot(first[2], three) + dot(first[1], slab(2, j)) + dot(first[0], one)
        upper[1 + j] = leaky(first_sum(whole)).astype(jnp.bfloat16)
        return first_sum(dot(first[1], slab(0, j)) + dot(first[2], one))

    rest_1 = first_layer(1)
    pl.semaphore_wait(
        barrier,
        count_space - 1 + has_left.astype(jnp.int32) + has_right.astype(jnp.int32),
    )

    @pl.when(has_up)
    def _():
        row_copy.start()
        upper_copy.start()

    @pl.when(has_right)
    def _():
        part_copies[1].start()

    @pl.when(has_down)
    def _():
        row_copy.wait_recv()

    rest_0 = first_layer(0)

    @pl.when(has_right)
    def _():
        part_copies[0].start()

    @pl.when(has_down)
    def _():
        upper_copy.wait_recv()

    high = upper[...].reshape(3 * upper.shape[1], upper.shape[2])
    sum_out[...] = deep_sum(dot(deep[0], high)).astype(jnp.bfloat16)

    @pl.when(has_right)
    def _():
        sum_copy.start()

    total = dot(deep[2], high)

    @pl.when(has_left)
    def _():
        part_copies[1].wait_recv()

    lower[2] = leaky(rest_1 + part_in[1].astype(jnp.float32)).astype(jnp.bfloat16)

    @pl.when(has_up)
    def _():
        lower_copy.start()

    @pl.when(has_left)
    def _():
        part_copies[0].wait_recv()

    lower[1] = leaky(rest_0 + part_in[0].astype(jnp.float32)).astype(jnp.bfloat16)

    @pl.when(has_down)
    def _():
        lower_copy.wait_recv()

    total = total + dot(deep[1], lower[...].reshape(3 * lower.shape[1], lower.shape[2]))
    total = deep_sum(total)

    @pl.when(has_left)
    def _():
        sum_copy.wait_recv()

    total = leaky(total + sum_in[...].astype(jnp.float32))
    for v in range(volumes):
        blocks_out[:, v, :] = total[:, v * lanes : (v + 1) * lanes]

    def block_copy(step):
        peer = lax.rem(me + step, count_space)
        return pltpu.make_async_remote_copy(
            src_ref=blocks_out.at[peer],
            dst_ref=blocks_in.at[me],
            send_sem=block_send.at[step],
            recv_sem=block_recv.at[step],
            device_id={"space": peer},
            device_id_type=MESH,
        )

    def block_start(step, carry):
        block_copy(step).start()
        return carry

    def block_wait(step, carry):
        block_copy(step).wait()
        return carry

    lax.fori_loop(1, count_space, block_start, 0)
    blocks_in[pl.ds(me, 1)] = blocks_out[pl.ds(me, 1)]

    @pl.when(has_up)
    def _():
        row_copy.wait_send()
        upper_copy.wait_send()
        lower_copy.wait_send()

    @pl.when(has_right)
    def _():
        part_copies[0].wait_send()
        part_copies[1].wait_send()
        sum_copy.wait_send()

    lax.fori_loop(1, count_space, block_wait, 0)
    for v in range(volumes):
        out[v] = blocks_in[:, v, :].astype(out.dtype)


def per_device(volumes, first_kernel, deep_kernel):
    count_space, count_filt = lax.axis_size("space"), lax.axis_size("filt")
    vols, size_x, size_y, channels, phases, lanes = volumes.shape
    cells = channels * phases
    filters = deep_kernel.shape[3]
    hidden = 2 * first_kernel.shape[3]
    wide = vols * lanes
    bf16, f32 = jnp.bfloat16, jnp.float32
    vmem = pl.BlockSpec(memory_space=pltpu.VMEM)
    out = pl.pallas_call(
        functools.partial(brick_kernel, count_space, count_filt),
        out_shape=jax.ShapeDtypeStruct((vols, count_space, lanes), bf16),
        in_specs=[vmem] * 3,
        out_specs=vmem,
        scratch_shapes=[
            pltpu.VMEM((vols, size_x, cells, lanes), bf16),
            pltpu.VMEM((3, hidden, wide), bf16),
            pltpu.VMEM((3, hidden, wide), bf16),
            pltpu.VMEM((2, hidden, wide), bf16),
            pltpu.VMEM((2, hidden, wide), bf16),
            pltpu.VMEM((filters, wide), bf16),
            pltpu.VMEM((filters, wide), bf16),
            pltpu.VMEM((filters, vols, lanes), f32),
            pltpu.VMEM((count_space, vols, lanes), f32),
            pltpu.SemaphoreType.DMA((6,)),
            pltpu.SemaphoreType.DMA((6,)),
            pltpu.SemaphoreType.DMA((count_space,)),
            pltpu.SemaphoreType.DMA((count_space,)),
        ],
        compiler_params=pltpu.CompilerParams(collective_id=0, has_side_effects=True),
        name="bricks",
    )(
        volumes.reshape(vols, size_x, size_y, cells, lanes),
        first_weights(first_kernel),
        deep_weights(deep_kernel),
    )
    return out.reshape(1, vols, 1, count_space, lanes)


def solution(mesh):
    in_specs = (P(None, "filt", "space", None, None, None), P(), P())
    out_specs = P("space", None, "filt", None, None)
    return jax.shard_map(
        per_device, mesh=mesh, in_specs=in_specs, out_specs=out_specs, check_vma=False
    )
```

```python
import functools

import jax
import jax.numpy as jnp
from jax import lax
from jax.experimental import pallas as pl
from jax.experimental.pallas import tpu as pltpu
from jax.sharding import PartitionSpec as P

MESH = pl.DeviceIdType.MESH
CORES, ROWS = 2, 8
CIN, C1 = 16, 32


def leaky(value):
    return jnp.where(value >= 0, value, 0.3 * value)


def placement(shape, period, group, phases):
    row = lax.broadcasted_iota(jnp.int32, shape, 0)
    column = lax.broadcasted_iota(jnp.int32, shape, 1)
    tap, channel = row // period, row % period
    role, rest = column // group, column % group
    if phases > 2:
        phase, own = rest % phases, rest // phases
    else:
        phase, own = rest // period, rest % period
    hit = jnp.logical_and(own == channel, phase == tap + 2 * role - 1)
    return jnp.where(hit, 1.0, 0.0).astype(jnp.bfloat16)


def place(raw, table, place_by, group):
    for a in range(3):
        for b in range(3):
            both = lax.dot_general(
                raw[a, b], place_by, (((0,), (0,)), ((), ())), preferred_element_type=jnp.float32
            ).astype(jnp.bfloat16)
            filters = both.shape[0]
            for role in range(both.shape[1] // group):
                table[a, role * filters : (role + 1) * filters, b * group : (b + 1) * group] = both[
                    :, role * group : (role + 1) * group
                ]


def shift_lane(value, lanes):
    parts = []
    for start in range(0, value.shape[1], lanes):
        part = pltpu.roll(value[:, start : start + lanes], 1, 1)
        lane = lax.broadcasted_iota(jnp.int32, part.shape, 1)
        parts.append(jnp.where(lane == 0, 0.0, part))
    return jnp.concatenate(parts, axis=1)


def dot(left, right):
    return jnp.dot(left, right, preferred_element_type=jnp.float32)


def brick_kernel(
    count_space,
    count_filt,
    vol_in,
    first_in,
    deep_in,
    out,
    vol,
    first_raw,
    deep_raw,
    first,
    deep,
    row,
    upper,
    lower,
    part_out,
    part_in,
    sum_out,
    sum_in,
    blocks_out,
    blocks_in,
    send_sem,
    recv_sem,
    block_send,
    block_recv,
    load_sem,
    known,
):
    volumes, _, _, cells, lanes = vol.shape
    me = lax.axis_index("space")
    column = lax.axis_index("filt")
    has_left, has_right = column > 0, column < count_filt - 1
    has_down, has_up = me > 0, me < count_space - 1
    barrier = pltpu.get_barrier_semaphore()
    core, y, z = me % CORES, (me // CORES) % ROWS, me // (CORES * ROWS)
    count_z = count_space // (CORES * ROWS)
    z_below, z_above = z > 0, z < count_z - 1
    partner = me + 1 - 2 * core
    across = me + 2 * core - 1
    has_across = jnp.logical_and(across >= 0, across < count_space)

    def beside(step):
        return z * (CORES * ROWS) + ((y + step + ROWS) % ROWS) * CORES + core

    def tell(semaphore, peer):
        pl.semaphore_signal(semaphore, inc=1, device_id={"space": peer}, device_id_type=MESH)

    def tell_z(semaphore):
        @pl.when(z_below)
        def _():
            tell(semaphore, me - CORES * ROWS)

        @pl.when(z_above)
        def _():
            tell(semaphore, me + CORES * ROWS)

    tell(barrier, partner)
    tell(barrier, beside(1))
    tell(barrier, beside(-1))
    tell_z(barrier)

    @pl.when(has_across)
    def _():
        tell(barrier, across)

    @pl.when(has_left)
    def _():
        pl.semaphore_signal(barrier, inc=1, device_id={"filt": column - 1}, device_id_type=MESH)

    @pl.when(has_right)
    def _():
        pl.semaphore_signal(barrier, inc=1, device_id={"filt": column + 1}, device_id_type=MESH)

    loads = [
        pltpu.make_async_copy(source, target, load_sem.at[which])
        for which, (source, target) in enumerate(
            [(first_in, first_raw), (vol_in, vol), (deep_in, deep_raw)]
        )
    ]
    for load in loads:
        load.start()

    def one(flag):
        return flag.astype(jnp.int32)

    z_peers = one(z_below) + one(z_above)

    def to_up(which, source, target):
        return pltpu.make_async_remote_copy(
            src_ref=source,
            dst_ref=target,
            send_sem=send_sem.at[which],
            recv_sem=recv_sem.at[which],
            device_id={"space": me + 1},
            device_id_type=MESH,
        )

    def to_right(which, source, target):
        return pltpu.make_async_remote_copy(
            src_ref=source,
            dst_ref=target,
            send_sem=send_sem.at[which],
            recv_sem=recv_sem.at[which],
            device_id={"filt": column + 1},
            device_id_type=MESH,
        )

    last = vol.shape[2] - 1
    row_copy = to_up(0, vol_in.at[:, :, last], row)
    upper_copy = to_up(1, upper.at[2], upper.at[0])
    lower_copy = to_up(2, lower.at[2], lower.at[0])
    part_copies = [to_right(3 + j, part_out.at[j], part_in.at[j]) for j in range(2)]
    sum_copy = to_right(5, sum_out, sum_in)

    @pl.when(jnp.logical_not(has_down))
    def _():
        row[...] = jnp.zeros_like(row)
        upper[0] = jnp.zeros(upper.shape[1:], upper.dtype)
        lower[0] = jnp.zeros(lower.shape[1:], lower.dtype)

    @pl.when(jnp.logical_not(has_left))
    def _():
        part_in[...] = jnp.zeros_like(part_in)
        sum_in[...] = jnp.zeros_like(sum_in)

    def slab(plane, j):
        sides = []
        for v in range(volumes):
            if j == 0:
                own = vol[v, plane, 0:2].reshape(2 * cells, lanes)
                sides.append(jnp.concatenate([row[v, plane], own], axis=0))
            else:
                sides.append(vol[v, plane, 1:4].reshape(3 * cells, lanes))
        return jnp.concatenate(sides, axis=1)

    def first_sum(value):
        third = value.shape[0] // 3
        even = value[:third] + shift_lane(value[2 * third :], lanes)
        return jnp.concatenate([even, value[third : 2 * third]], axis=0)

    def deep_sum(value):
        half = value.shape[0] // 2
        return value[:half] + shift_lane(value[half:], lanes)

    def first_layer(j):
        three = slab(3, j)
        part_out[j] = first_sum(dot(first[0], three)).astype(jnp.bfloat16)
        one = slab(1, j)
        whole = dot(first[2], three) + dot(first[1], slab(2, j)) + dot(first[0], one)
        upper[1 + j] = leaky(first_sum(whole)).astype(jnp.bfloat16)
        return first_sum(dot(first[1], slab(0, j)) + dot(first[2], one))

    pl.semaphore_wait(barrier, 3 + z_peers + one(has_across) + one(has_left) + one(has_right))

    @pl.when(has_up)
    def _():
        row_copy.start()

    tell(known.at[0], beside(1))
    tell(known.at[0], beside(-1))
    loads[0].wait()
    place(first_raw, first, placement((3 * CIN, 3 * 4 * CIN), CIN, 4 * CIN, 4), 4 * CIN)
    pl.semaphore_wait(known.at[0], 2)
    tell(known.at[1], beside(2))
    tell(known.at[1], beside(-2))
    loads[1].wait()
    rest_1 = first_layer(1)

    @pl.when(has_up)
    def _():
        upper_copy.start()

    @pl.when(has_right)
    def _():
        part_copies[1].start()

    loads[2].wait()
    place(deep_raw, deep, placement((3 * C1, 4 * C1), C1, 2 * C1, 2), 2 * C1)
    pl.semaphore_wait(known.at[1], 2)
    tell_z(known.at[2])

    @pl.when(has_down)
    def _():
        row_copy.wait_recv()

    rest_0 = first_layer(0)

    @pl.when(has_right)
    def _():
        part_copies[0].start()

    @pl.when(has_down)
    def _():
        upper_copy.wait_recv()

    high = upper[...].reshape(3 * upper.shape[1], upper.shape[2])
    sum_out[...] = deep_sum(dot(deep[0], high)).astype(jnp.bfloat16)

    @pl.when(has_right)
    def _():
        sum_copy.start()

    total = dot(deep[2], high)
    pl.semaphore_wait(known.at[2], z_peers)
    tell(known.at[3], (z + count_z // 2) % count_z * (CORES * ROWS) + me % (CORES * ROWS))

    @pl.when(has_left)
    def _():
        part_copies[1].wait_recv()

    lower[2] = leaky(rest_1 + part_in[1].astype(jnp.float32)).astype(jnp.bfloat16)

    @pl.when(has_up)
    def _():
        lower_copy.start()

    pl.semaphore_wait(known.at[3], 1)
    tell(known.at[4], partner)

    @pl.when(has_left)
    def _():
        part_copies[0].wait_recv()

    lower[1] = leaky(rest_0 + part_in[0].astype(jnp.float32)).astype(jnp.bfloat16)

    @pl.when(has_down)
    def _():
        lower_copy.wait_recv()

    total = total + dot(deep[1], lower[...].reshape(3 * lower.shape[1], lower.shape[2]))
    total = deep_sum(total)

    @pl.when(has_left)
    def _():
        sum_copy.wait_recv()

    total = leaky(total + sum_in[...].astype(jnp.float32))
    for v in range(volumes):
        blocks_out[:, v, :] = total[:, v * lanes : (v + 1) * lanes]

    def block_copy(step):
        peer = lax.rem(me + step, count_space)
        return pltpu.make_async_remote_copy(
            src_ref=blocks_out.at[peer],
            dst_ref=blocks_in.at[me],
            send_sem=block_send.at[step],
            recv_sem=block_recv.at[step],
            device_id={"space": peer},
            device_id_type=MESH,
        )

    def block_start(step, carry):
        block_copy(step).start()
        return carry

    def block_wait(step, carry):
        block_copy(step).wait()
        return carry

    pl.semaphore_wait(known.at[4], 1)
    lax.fori_loop(1, count_space, block_start, 0)
    blocks_in[pl.ds(me, 1)] = blocks_out[pl.ds(me, 1)]

    @pl.when(has_up)
    def _():
        row_copy.wait_send()
        upper_copy.wait_send()
        lower_copy.wait_send()

    @pl.when(has_right)
    def _():
        part_copies[0].wait_send()
        part_copies[1].wait_send()
        sum_copy.wait_send()

    lax.fori_loop(1, count_space, block_wait, 0)
    for v in range(volumes):
        out[v] = blocks_in[:, v, :].astype(out.dtype)


def per_device(volumes, first_kernel, deep_kernel):
    count_space, count_filt = lax.axis_size("space"), lax.axis_size("filt")
    vols, size_x, size_y, channels, phases, lanes = volumes.shape
    cells = channels * phases
    filters = deep_kernel.shape[3]
    hidden = 2 * first_kernel.shape[3]
    wide = vols * lanes
    bf16, f32 = jnp.bfloat16, jnp.float32
    vmem = pl.BlockSpec(memory_space=pltpu.VMEM)
    out = pl.pallas_call(
        functools.partial(brick_kernel, count_space, count_filt),
        out_shape=jax.ShapeDtypeStruct((vols, count_space, lanes), bf16),
        in_specs=[pl.BlockSpec(memory_space=pltpu.MemorySpace.HBM)] * 3,
        out_specs=vmem,
        scratch_shapes=[
            pltpu.VMEM((vols, size_x, size_y, cells, lanes), bf16),
            pltpu.VMEM((3, 3, 3 * channels, hidden // 2), bf16),
            pltpu.VMEM((3, 3, 3 * hidden // 2, filters), bf16),
            pltpu.VMEM((3, 3 * hidden // 2, 3 * cells), bf16),
            pltpu.VMEM((3, 2 * filters, 3 * hidden), bf16),
            pltpu.VMEM((vols, size_x, cells, lanes), bf16),
            pltpu.VMEM((3, hidden, wide), bf16),
            pltpu.VMEM((3, hidden, wide), bf16),
            pltpu.VMEM((2, hidden, wide), bf16),
            pltpu.VMEM((2, hidden, wide), bf16),
            pltpu.VMEM((filters, wide), bf16),
            pltpu.VMEM((filters, wide), bf16),
            pltpu.VMEM((filters, vols, lanes), f32),
            pltpu.VMEM((count_space, vols, lanes), f32),
            pltpu.SemaphoreType.DMA((6,)),
            pltpu.SemaphoreType.DMA((6,)),
            pltpu.SemaphoreType.DMA((count_space,)),
            pltpu.SemaphoreType.DMA((count_space,)),
            pltpu.SemaphoreType.DMA((3,)),
            pltpu.SemaphoreType.REGULAR((5,)),
        ],
        compiler_params=pltpu.CompilerParams(
            collective_id=0, has_side_effects=True
        ),
        name="bricks",
    )(
        volumes.reshape(vols, size_x, size_y, cells, lanes),
        jnp.swapaxes(first_kernel, 3, 4).reshape(3, 3, 3 * channels, hidden // 2),
        jnp.swapaxes(deep_kernel, 3, 4).reshape(3, 3, 3 * hidden // 2, filters),
    )
    return out.reshape(1, vols, 1, count_space, lanes)


def solution(mesh):
    in_specs = (P(None, "filt", "space", None, None, None), P(), P())
    out_specs = P("space", None, "filt", None, None)
    return jax.shard_map(
        per_device, mesh=mesh, in_specs=in_specs, out_specs=out_specs, check_vma=False
    )
```

```python
import functools

import jax
import jax.numpy as jnp
from jax import lax
from jax.experimental import pallas as pl
from jax.experimental.pallas import tpu as pltpu
from jax.sharding import PartitionSpec as P

MESH = pl.DeviceIdType.MESH
CORES, ROWS = 2, 8
CIN, C1 = 16, 32


def leaky(value):
    return jnp.where(value >= 0, value, 0.3 * value)


def placement(shape, period, group, phases):
    row = lax.broadcasted_iota(jnp.int32, shape, 0)
    column = lax.broadcasted_iota(jnp.int32, shape, 1)
    tap, channel = row // period, row % period
    role, rest = column // group, column % group
    if phases > 2:
        phase, own = rest % phases, rest // phases
    else:
        phase, own = rest // period, rest % period
    hit = jnp.logical_and(own == channel, phase == tap + 2 * role - 1)
    return jnp.where(hit, 1.0, 0.0).astype(jnp.bfloat16)


def place(raw, table, place_by, group, taps_x):
    for a in taps_x:
        for b in range(3):
            both = lax.dot_general(
                raw[a, b], place_by, (((0,), (0,)), ((), ())), preferred_element_type=jnp.float32
            ).astype(jnp.bfloat16)
            filters = both.shape[0]
            for role in range(both.shape[1] // group):
                table[a, role * filters : (role + 1) * filters, b * group : (b + 1) * group] = both[
                    :, role * group : (role + 1) * group
                ]


def shift_lane(value, lanes):
    parts = []
    for start in range(0, value.shape[1], lanes):
        part = pltpu.roll(value[:, start : start + lanes], 1, 1)
        lane = lax.broadcasted_iota(jnp.int32, part.shape, 1)
        parts.append(jnp.where(lane == 0, 0.0, part))
    return jnp.concatenate(parts, axis=1)


def dot(left, right):
    return jnp.dot(left, right, preferred_element_type=jnp.float32)


def brick_kernel(
    count_space,
    count_filt,
    vol_in,
    first_in,
    deep_in,
    out,
    vol,
    first_raw,
    deep_raw,
    first,
    deep,
    row,
    upper,
    lower,
    part_out,
    part_in,
    sum_out,
    sum_in,
    blocks_out,
    blocks_in,
    send_sem,
    recv_sem,
    block_send,
    block_recv,
    load_sem,
    known,
):
    volumes, _, _, cells, lanes = vol.shape
    me = lax.axis_index("space")
    column = lax.axis_index("filt")
    has_left, has_right = column > 0, column < count_filt - 1
    has_down, has_up = me > 0, me < count_space - 1
    barrier = pltpu.get_barrier_semaphore()
    core, y, z = me % CORES, (me // CORES) % ROWS, me // (CORES * ROWS)
    count_z = count_space // (CORES * ROWS)
    z_below, z_above = z > 0, z < count_z - 1
    partner = me + 1 - 2 * core
    across = me + 2 * core - 1
    has_across = jnp.logical_and(across >= 0, across < count_space)

    def beside(step):
        return z * (CORES * ROWS) + ((y + step + ROWS) % ROWS) * CORES + core

    def tell(semaphore, peer):
        pl.semaphore_signal(semaphore, inc=1, device_id={"space": peer}, device_id_type=MESH)

    def tell_z(semaphore):
        @pl.when(z_below)
        def _():
            tell(semaphore, me - CORES * ROWS)

        @pl.when(z_above)
        def _():
            tell(semaphore, me + CORES * ROWS)

    tell(barrier, partner)
    tell(barrier, beside(1))
    tell(barrier, beside(-1))
    tell_z(barrier)

    @pl.when(has_across)
    def _():
        tell(barrier, across)

    @pl.when(has_left)
    def _():
        pl.semaphore_signal(barrier, inc=1, device_id={"filt": column - 1}, device_id_type=MESH)

    @pl.when(has_right)
    def _():
        pl.semaphore_signal(barrier, inc=1, device_id={"filt": column + 1}, device_id_type=MESH)

    loads = [
        pltpu.make_async_copy(source, target, load_sem.at[which])
        for which, (source, target) in enumerate(
            [(first_in, first_raw), (vol_in, vol), (deep_in, deep_raw)]
        )
    ]
    for load in loads:
        load.start()

    def one(flag):
        return flag.astype(jnp.int32)

    z_peers = one(z_below) + one(z_above)

    def to_up(which, source, target):
        return pltpu.make_async_remote_copy(
            src_ref=source,
            dst_ref=target,
            send_sem=send_sem.at[which],
            recv_sem=recv_sem.at[which],
            device_id={"space": me + 1},
            device_id_type=MESH,
        )

    def to_right(which, source, target):
        return pltpu.make_async_remote_copy(
            src_ref=source,
            dst_ref=target,
            send_sem=send_sem.at[which],
            recv_sem=recv_sem.at[which],
            device_id={"filt": column + 1},
            device_id_type=MESH,
        )

    last = vol.shape[2] - 1
    row_copy = to_up(0, vol_in.at[:, :, last], row)
    upper_copy = to_up(1, upper.at[2], upper.at[0])
    lower_copy = to_up(2, lower.at[2], lower.at[0])
    part_copies = [to_right(3 + j, part_out.at[j], part_in.at[j]) for j in range(2)]
    sum_copy = to_right(5, sum_out, sum_in)

    @pl.when(jnp.logical_not(has_down))
    def _():
        row[...] = jnp.zeros_like(row)
        upper[0] = jnp.zeros(upper.shape[1:], upper.dtype)
        lower[0] = jnp.zeros(lower.shape[1:], lower.dtype)

    @pl.when(jnp.logical_not(has_left))
    def _():
        part_in[...] = jnp.zeros_like(part_in)
        sum_in[...] = jnp.zeros_like(sum_in)

    def slab(plane, j):
        sides = []
        for v in range(volumes):
            if j == 0:
                own = vol[v, plane, 0:2].reshape(2 * cells, lanes)
                sides.append(jnp.concatenate([row[v, plane], own], axis=0))
            else:
                sides.append(vol[v, plane, 1:4].reshape(3 * cells, lanes))
        return jnp.concatenate(sides, axis=1)

    def first_sum(value):
        third = value.shape[0] // 3
        even = value[:third] + shift_lane(value[2 * third :], lanes)
        return jnp.concatenate([even, value[third : 2 * third]], axis=0)

    def deep_sum(value):
        half = value.shape[0] // 2
        return value[:half] + shift_lane(value[half:], lanes)

    def first_part(j):
        three = slab(3, j)
        part_out[j] = first_sum(dot(first[0], three)).astype(jnp.bfloat16)
        return three

    def first_upper(j, three):
        whole = dot(first[2], three) + dot(first[1], slab(2, j)) + dot(first[0], slab(1, j))
        upper[1 + j] = leaky(first_sum(whole)).astype(jnp.bfloat16)

    def first_rest(j):
        return first_sum(dot(first[1], slab(0, j)) + dot(first[2], slab(1, j)))

    pl.semaphore_wait(barrier, 3 + z_peers + one(has_across) + one(has_left) + one(has_right))

    @pl.when(has_up)
    def _():
        row_copy.start()

    tell(known.at[0], beside(1))
    tell(known.at[0], beside(-1))
    loads[0].wait()
    spots = placement((3 * CIN, 3 * 4 * CIN), CIN, 4 * CIN, 4)
    place(first_raw, first, spots, 4 * CIN, (0,))
    loads[1].wait()
    three = first_part(1)

    @pl.when(has_right)
    def _():
        part_copies[1].start()

    pl.semaphore_wait(known.at[0], 2)
    tell(known.at[1], beside(2))
    tell(known.at[1], beside(-2))
    place(first_raw, first, spots, 4 * CIN, (1, 2))
    first_upper(1, three)

    @pl.when(has_up)
    def _():
        upper_copy.start()

    @pl.when(has_down)
    def _():
        row_copy.wait_recv()

    three = first_part(0)

    @pl.when(has_right)
    def _():
        part_copies[0].start()

    pl.semaphore_wait(known.at[1], 2)
    tell_z(known.at[2])
    first_upper(0, three)
    loads[2].wait()
    spots = placement((3 * C1, 4 * C1), C1, 2 * C1, 2)
    place(deep_raw, deep, spots, 2 * C1, (0,))

    @pl.when(has_down)
    def _():
        upper_copy.wait_recv()

    high = upper[...].reshape(3 * upper.shape[1], upper.shape[2])
    sum_out[...] = deep_sum(dot(deep[0], high)).astype(jnp.bfloat16)

    @pl.when(has_right)
    def _():
        sum_copy.start()

    place(deep_raw, deep, spots, 2 * C1, (1, 2))
    rest_1, rest_0 = first_rest(1), first_rest(0)
    total = dot(deep[2], high)
    pl.semaphore_wait(known.at[2], z_peers)
    tell(known.at[3], (z + count_z // 2) % count_z * (CORES * ROWS) + me % (CORES * ROWS))

    @pl.when(has_left)
    def _():
        part_copies[1].wait_recv()

    lower[2] = leaky(rest_1 + part_in[1].astype(jnp.float32)).astype(jnp.bfloat16)

    @pl.when(has_up)
    def _():
        lower_copy.start()

    pl.semaphore_wait(known.at[3], 1)
    tell(known.at[4], partner)

    @pl.when(has_left)
    def _():
        part_copies[0].wait_recv()

    lower[1] = leaky(rest_0 + part_in[0].astype(jnp.float32)).astype(jnp.bfloat16)

    @pl.when(has_down)
    def _():
        lower_copy.wait_recv()

    total = total + dot(deep[1], lower[...].reshape(3 * lower.shape[1], lower.shape[2]))
    total = deep_sum(total)

    @pl.when(has_left)
    def _():
        sum_copy.wait_recv()

    total = leaky(total + sum_in[...].astype(jnp.float32))
    blocks_out[...] = jnp.stack(
        [total[:, v * lanes : (v + 1) * lanes] for v in range(volumes)], axis=1
    ).astype(jnp.bfloat16)

    turn = jnp.where(z < count_z // 2, 1, -1)

    def block_copy(source, target, peer):
        return pltpu.make_async_remote_copy(
            src_ref=source,
            dst_ref=target,
            send_sem=block_send,
            recv_sem=block_recv,
            device_id={"space": peer},
            device_id_type=MESH,
        )

    strides = next(n for n in (7, 3, 1) if (count_space - 1) % n == 0)

    def block_starts(step, carry):
        for k in range(strides):
            away = turn * (count_space - 1 - step * strides - k)
            peer = lax.rem(me + count_space + away, count_space)
            block_copy(blocks_out.at[peer], blocks_in.at[me], peer).start()
        return carry

    pl.semaphore_wait(known.at[4], 1)
    lax.fori_loop(0, (count_space - 1) // strides, block_starts, 0)
    blocks_in[pl.ds(me, 1)] = blocks_out[pl.ds(me, 1)]

    @pl.when(has_up)
    def _():
        row_copy.wait_send()
        upper_copy.wait_send()
        lower_copy.wait_send()

    @pl.when(has_right)
    def _():
        part_copies[0].wait_send()
        part_copies[1].wait_send()
        sum_copy.wait_send()

    others = pl.ds(0, count_space - 1)
    block_copy(blocks_out.at[others], blocks_in.at[others], partner).wait()
    whole = blocks_in[...].astype(jnp.float32)
    for v in range(volumes):
        out[v] = whole[:, v, :].astype(out.dtype)


def per_device(volumes, first_kernel, deep_kernel):
    count_space, count_filt = lax.axis_size("space"), lax.axis_size("filt")
    vols, size_x, size_y, channels, phases, lanes = volumes.shape
    cells = channels * phases
    filters = deep_kernel.shape[3]
    hidden = 2 * first_kernel.shape[3]
    wide = vols * lanes
    bf16, f32 = jnp.bfloat16, jnp.float32
    vmem = pl.BlockSpec(memory_space=pltpu.VMEM)
    out = pl.pallas_call(
        functools.partial(brick_kernel, count_space, count_filt),
        out_shape=pltpu.VMEM((vols, count_space, lanes), bf16),
        in_specs=[pl.BlockSpec(memory_space=pltpu.MemorySpace.HBM)] * 3,
        out_specs=vmem,
        scratch_shapes=[
            pltpu.VMEM((vols, size_x, size_y, cells, lanes), bf16),
            pltpu.VMEM((3, 3, 3 * channels, hidden // 2), bf16),
            pltpu.VMEM((3, 3, 3 * hidden // 2, filters), bf16),
            pltpu.VMEM((3, 3 * hidden // 2, 3 * cells), bf16),
            pltpu.VMEM((3, 2 * filters, 3 * hidden), bf16),
            pltpu.VMEM((vols, size_x, cells, lanes), bf16),
            pltpu.VMEM((3, hidden, wide), bf16),
            pltpu.VMEM((3, hidden, wide), bf16),
            pltpu.VMEM((2, hidden, wide), bf16),
            pltpu.VMEM((2, hidden, wide), bf16),
            pltpu.VMEM((filters, wide), bf16),
            pltpu.VMEM((filters, wide), bf16),
            pltpu.VMEM((filters, vols, lanes), bf16),
            pltpu.VMEM((count_space, vols, lanes), bf16),
            pltpu.SemaphoreType.DMA((6,)),
            pltpu.SemaphoreType.DMA((6,)),
            pltpu.SemaphoreType.DMA,
            pltpu.SemaphoreType.DMA,
            pltpu.SemaphoreType.DMA((3,)),
            pltpu.SemaphoreType.REGULAR((5,)),
        ],
        compiler_params=pltpu.CompilerParams(
            collective_id=0, has_side_effects=True
        ),
        name="bricks",
    )(
        volumes.reshape(vols, size_x, size_y, cells, lanes),
        jnp.swapaxes(first_kernel, 3, 4).reshape(3, 3, 3 * channels, hidden // 2),
        jnp.swapaxes(deep_kernel, 3, 4).reshape(3, 3, 3 * hidden // 2, filters),
    )
    return out.reshape(1, vols, 1, count_space, lanes)


def solution(mesh):
    in_specs = (P(None, "filt", "space", None, None, None), P(), P())
    out_specs = P("space", None, "filt", None, None)
    return jax.shard_map(
        per_device, mesh=mesh, in_specs=in_specs, out_specs=out_specs, check_vma=False
    )
```

```python
import functools

import jax
import jax.numpy as jnp
from jax import lax
from jax.experimental import pallas as pl
from jax.experimental.pallas import tpu as pltpu
from jax.sharding import PartitionSpec as P

MESH = pl.DeviceIdType.MESH
CORES, ROWS = 2, 8
CIN, C1 = 16, 32


def leaky(value):
    return jnp.where(value >= 0, value, 0.3 * value)


def placement(shape, period, group, phases):
    row = lax.broadcasted_iota(jnp.int32, shape, 0)
    column = lax.broadcasted_iota(jnp.int32, shape, 1)
    tap, channel = row // period, row % period
    role, rest = column // group, column % group
    if phases > 2:
        phase, own = rest % phases, rest // phases
    else:
        phase, own = rest // period, rest % period
    hit = jnp.logical_and(own == channel, phase == tap + 2 * role - 1)
    return jnp.where(hit, 1.0, 0.0).astype(jnp.bfloat16)


def place(raw, table, place_by, group, taps_x):
    for a in taps_x:
        for b in range(3):
            both = lax.dot_general(
                raw[a, b], place_by, (((0,), (0,)), ((), ())), preferred_element_type=jnp.float32
            ).astype(jnp.bfloat16)
            filters = both.shape[0]
            for role in range(both.shape[1] // group):
                table[a, role * filters : (role + 1) * filters, b * group : (b + 1) * group] = both[
                    :, role * group : (role + 1) * group
                ]


def shift_lane(value, lanes):
    parts = []
    for start in range(0, value.shape[1], lanes):
        part = pltpu.roll(value[:, start : start + lanes], 1, 1)
        lane = lax.broadcasted_iota(jnp.int32, part.shape, 1)
        parts.append(jnp.where(lane == 0, 0.0, part))
    return jnp.concatenate(parts, axis=1)


def dot(left, right):
    return jnp.dot(left, right, preferred_element_type=jnp.float32)


def brick_kernel(
    count_space,
    count_filt,
    vol_in,
    first_in,
    deep_in,
    out,
    vol,
    first_raw,
    deep_raw,
    first,
    deep,
    row,
    upper,
    lower,
    part_out,
    part_in,
    sum_out,
    sum_in,
    blocks_out,
    blocks_in,
    send_sem,
    recv_sem,
    block_send,
    block_recv,
    load_sem,
    known,
):
    volumes, _, _, cells, lanes = vol.shape
    me = lax.axis_index("space")
    column = lax.axis_index("filt")
    has_left, has_right = column > 0, column < count_filt - 1
    has_down, has_up = me > 0, me < count_space - 1
    barrier = pltpu.get_barrier_semaphore()
    core, y, z = me % CORES, (me // CORES) % ROWS, me // (CORES * ROWS)
    count_z = count_space // (CORES * ROWS)
    z_below, z_above = z > 0, z < count_z - 1
    partner = me + 1 - 2 * core
    across = me + 2 * core - 1
    has_across = jnp.logical_and(across >= 0, across < count_space)

    def beside(step):
        return z * (CORES * ROWS) + ((y + step + ROWS) % ROWS) * CORES + core

    def tell(semaphore, peer):
        pl.semaphore_signal(semaphore, inc=1, device_id={"space": peer}, device_id_type=MESH)

    def tell_z(semaphore):
        @pl.when(z_below)
        def _():
            tell(semaphore, me - CORES * ROWS)

        @pl.when(z_above)
        def _():
            tell(semaphore, me + CORES * ROWS)

    tell(barrier, partner)
    tell(barrier, beside(1))
    tell(barrier, beside(-1))
    tell_z(barrier)

    @pl.when(has_across)
    def _():
        tell(barrier, across)

    @pl.when(has_left)
    def _():
        pl.semaphore_signal(barrier, inc=1, device_id={"filt": column - 1}, device_id_type=MESH)

    @pl.when(has_right)
    def _():
        pl.semaphore_signal(barrier, inc=1, device_id={"filt": column + 1}, device_id_type=MESH)

    loads = [
        pltpu.make_async_copy(source, target, load_sem.at[which])
        for which, (source, target) in enumerate(
            [(first_in, first_raw), (vol_in, vol), (deep_in, deep_raw)]
        )
    ]
    for load in loads:
        load.start()

    def one(flag):
        return flag.astype(jnp.int32)

    z_peers = one(z_below) + one(z_above)

    def to_up(which, source, target):
        return pltpu.make_async_remote_copy(
            src_ref=source,
            dst_ref=target,
            send_sem=send_sem.at[which],
            recv_sem=recv_sem.at[which],
            device_id={"space": me + 1},
            device_id_type=MESH,
        )

    def to_right(which, source, target):
        return pltpu.make_async_remote_copy(
            src_ref=source,
            dst_ref=target,
            send_sem=send_sem.at[which],
            recv_sem=recv_sem.at[which],
            device_id={"filt": column + 1},
            device_id_type=MESH,
        )

    last = vol.shape[2] - 1
    row_copy = to_up(0, vol_in.at[:, :, last], row)
    upper_copy = to_up(1, upper.at[2], upper.at[0])
    lower_copy = to_up(2, lower.at[2], lower.at[0])
    part_copies = [to_right(3 + j, part_out.at[j], part_in.at[j]) for j in range(2)]
    sum_copy = to_right(5, sum_out, sum_in)

    @pl.when(jnp.logical_not(has_down))
    def _():
        row[...] = jnp.zeros_like(row)
        upper[0] = jnp.zeros(upper.shape[1:], upper.dtype)
        lower[0] = jnp.zeros(lower.shape[1:], lower.dtype)

    @pl.when(jnp.logical_not(has_left))
    def _():
        part_in[...] = jnp.zeros_like(part_in)
        sum_in[...] = jnp.zeros_like(sum_in)

    def slab(plane, j):
        sides = []
        for v in range(volumes):
            if j == 0:
                own = vol[v, plane, 0:2].reshape(2 * cells, lanes)
                sides.append(jnp.concatenate([row[v, plane], own], axis=0))
            else:
                sides.append(vol[v, plane, 1:4].reshape(3 * cells, lanes))
        return jnp.concatenate(sides, axis=1)

    def first_sum(value):
        third = value.shape[0] // 3
        even = value[:third] + shift_lane(value[2 * third :], lanes)
        return jnp.concatenate([even, value[third : 2 * third]], axis=0)

    def deep_sum(value):
        half = value.shape[0] // 2
        return value[:half] + shift_lane(value[half:], lanes)

    def first_part(j):
        three = slab(3, j)
        part_out[j] = first_sum(dot(first[0], three)).astype(jnp.bfloat16)
        return three

    def first_upper(j, three):
        whole = dot(first[2], three) + dot(first[1], slab(2, j)) + dot(first[0], slab(1, j))
        upper[1 + j] = leaky(first_sum(whole)).astype(jnp.bfloat16)

    def first_rest(j):
        return first_sum(dot(first[1], slab(0, j)) + dot(first[2], slab(1, j)))

    loads[0].wait()
    spots = placement((3 * CIN, 3 * 4 * CIN), CIN, 4 * CIN, 4)
    place(first_raw, first, spots, 4 * CIN, (0,))
    loads[1].wait()
    three = first_part(1)

    pl.semaphore_wait(barrier, 3 + z_peers + one(has_across) + one(has_left) + one(has_right))

    @pl.when(has_up)
    def _():
        row_copy.start()

    tell(known.at[0], beside(1))
    tell(known.at[0], beside(-1))
    @pl.when(has_right)
    def _():
        part_copies[1].start()

    pl.semaphore_wait(known.at[0], 2)
    tell(known.at[1], beside(2))
    tell(known.at[1], beside(-2))
    place(first_raw, first, spots, 4 * CIN, (1, 2))
    first_upper(1, three)

    @pl.when(has_up)
    def _():
        upper_copy.start()

    @pl.when(has_down)
    def _():
        row_copy.wait_recv()

    three = first_part(0)

    @pl.when(has_right)
    def _():
        part_copies[0].start()

    pl.semaphore_wait(known.at[1], 2)
    tell_z(known.at[2])
    first_upper(0, three)
    loads[2].wait()
    spots = placement((3 * C1, 4 * C1), C1, 2 * C1, 2)
    place(deep_raw, deep, spots, 2 * C1, (0,))

    @pl.when(has_down)
    def _():
        upper_copy.wait_recv()

    high = upper[...].reshape(3 * upper.shape[1], upper.shape[2])
    sum_out[...] = deep_sum(dot(deep[0], high)).astype(jnp.bfloat16)

    @pl.when(has_right)
    def _():
        sum_copy.start()

    place(deep_raw, deep, spots, 2 * C1, (1, 2))
    rest_1, rest_0 = first_rest(1), first_rest(0)
    total = dot(deep[2], high)
    pl.semaphore_wait(known.at[2], z_peers)
    tell(known.at[3], (z + count_z // 2) % count_z * (CORES * ROWS) + me % (CORES * ROWS))

    @pl.when(has_left)
    def _():
        part_copies[1].wait_recv()

    lower[2] = leaky(rest_1 + part_in[1].astype(jnp.float32)).astype(jnp.bfloat16)

    @pl.when(has_up)
    def _():
        lower_copy.start()

    pl.semaphore_wait(known.at[3], 1)
    tell(known.at[4], partner)

    @pl.when(has_left)
    def _():
        part_copies[0].wait_recv()

    lower[1] = leaky(rest_0 + part_in[0].astype(jnp.float32)).astype(jnp.bfloat16)

    @pl.when(has_down)
    def _():
        lower_copy.wait_recv()

    total = total + dot(deep[1], lower[...].reshape(3 * lower.shape[1], lower.shape[2]))
    total = deep_sum(total)

    @pl.when(has_left)
    def _():
        sum_copy.wait_recv()

    total = leaky(total + sum_in[...].astype(jnp.float32))
    blocks_out[...] = jnp.stack(
        [total[:, v * lanes : (v + 1) * lanes] for v in range(volumes)], axis=1
    ).astype(jnp.bfloat16)

    turn = jnp.where(z < count_z // 2, 1, -1)

    def block_copy(source, target, peer):
        return pltpu.make_async_remote_copy(
            src_ref=source,
            dst_ref=target,
            send_sem=block_send,
            recv_sem=block_recv,
            device_id={"space": peer},
            device_id_type=MESH,
        )

    strides = next(n for n in (7, 3, 1) if (count_space - 1) % n == 0)

    def block_starts(step, carry):
        for k in range(strides):
            away = turn * (count_space - 1 - step * strides - k)
            peer = lax.rem(me + count_space + away, count_space)
            block_copy(blocks_out.at[peer], blocks_in.at[me], peer).start()
        return carry

    pl.semaphore_wait(known.at[4], 1)
    lax.fori_loop(0, (count_space - 1) // strides, block_starts, 0)
    blocks_in[pl.ds(me, 1)] = blocks_out[pl.ds(me, 1)]

    @pl.when(has_up)
    def _():
        row_copy.wait_send()
        upper_copy.wait_send()
        lower_copy.wait_send()

    @pl.when(has_right)
    def _():
        part_copies[0].wait_send()
        part_copies[1].wait_send()
        sum_copy.wait_send()

    others = pl.ds(0, count_space - 1)
    block_copy(blocks_out.at[others], blocks_in.at[others], partner).wait()
    whole = blocks_in[...].astype(jnp.float32)
    for v in range(volumes):
        out[v] = whole[:, v, :].astype(out.dtype)


def per_device(volumes, first_kernel, deep_kernel):
    count_space, count_filt = lax.axis_size("space"), lax.axis_size("filt")
    vols, size_x, size_y, channels, phases, lanes = volumes.shape
    cells = channels * phases
    filters = deep_kernel.shape[3]
    hidden = 2 * first_kernel.shape[3]
    wide = vols * lanes
    bf16, f32 = jnp.bfloat16, jnp.float32
    vmem = pl.BlockSpec(memory_space=pltpu.VMEM)
    out = pl.pallas_call(
        functools.partial(brick_kernel, count_space, count_filt),
        out_shape=pltpu.VMEM((vols, count_space, lanes), bf16),
        in_specs=[pl.BlockSpec(memory_space=pltpu.MemorySpace.HBM)] * 3,
        out_specs=vmem,
        scratch_shapes=[
            pltpu.VMEM((vols, size_x, size_y, cells, lanes), bf16),
            pltpu.VMEM((3, 3, 3 * channels, hidden // 2), bf16),
            pltpu.VMEM((3, 3, 3 * hidden // 2, filters), bf16),
            pltpu.VMEM((3, 3 * hidden // 2, 3 * cells), bf16),
            pltpu.VMEM((3, 2 * filters, 3 * hidden), bf16),
            pltpu.VMEM((vols, size_x, cells, lanes), bf16),
            pltpu.VMEM((3, hidden, wide), bf16),
            pltpu.VMEM((3, hidden, wide), bf16),
            pltpu.VMEM((2, hidden, wide), bf16),
            pltpu.VMEM((2, hidden, wide), bf16),
            pltpu.VMEM((filters, wide), bf16),
            pltpu.VMEM((filters, wide), bf16),
            pltpu.VMEM((filters, vols, lanes), bf16),
            pltpu.VMEM((count_space, vols, lanes), bf16),
            pltpu.SemaphoreType.DMA((6,)),
            pltpu.SemaphoreType.DMA((6,)),
            pltpu.SemaphoreType.DMA,
            pltpu.SemaphoreType.DMA,
            pltpu.SemaphoreType.DMA((3,)),
            pltpu.SemaphoreType.REGULAR((5,)),
        ],
        compiler_params=pltpu.CompilerParams(
            collective_id=0, has_side_effects=True
        ),
        name="bricks",
    )(
        volumes.reshape(vols, size_x, size_y, cells, lanes),
        jnp.swapaxes(first_kernel, 3, 4).reshape(3, 3, 3 * channels, hidden // 2),
        jnp.swapaxes(deep_kernel, 3, 4).reshape(3, 3, 3 * hidden // 2, filters),
    )
    return out.reshape(1, vols, 1, count_space, lanes)


def solution(mesh):
    in_specs = (P(None, "filt", "space", None, None, None), P(), P())
    out_specs = P("space", None, "filt", None, None)
    return jax.shard_map(
        per_device, mesh=mesh, in_specs=in_specs, out_specs=out_specs, check_vma=False
    )
```
